32 devices in a mesh: freq: 8 (over y, x, core), recv: 4 (over z).
Axes of the slice: x: 2, y: 2, z: 4, core: 2. Of those that a mesh axis runs over, the one named last changes fastest.
Arguments:
- response: bfloat16 [2, 256, 128, 4096], P(None, 'freq', 'recv'), may hold values from -0.0625 to 0.0625
- focusing: float32 [2, 256, 16, 4096], P(None, 'freq', None, 'recv'), may hold values from -6 to 6
- window_onset: int32 [16, 128], P(None, ('recv', 'freq')), may hold values from 0 to 511
- window_end: int32 [16, 128], P(None, ('recv', 'freq')), may hold values from 128 to 1023, as said below
Outputs:
- windowed: float32 [16, 128, 1024], P(None, ('recv', 'freq'))
The draws below stay inside these ranges and needn't reach their ends.
Inputs may be any that keep to these rules, and one draw needn't show every extreme that they name: window_end - window_onset lies between 128 and 512 for every trace.
All inputs are finite; a program needn't handle non-finite values.
Results may differ from the reference program's by a relative error of at most 0.0029.
Values may be sent and summed in bfloat16 or wider, within the bound.
A program may use at most 64 MiB of HBM per device.

```python
import math
import jax
import jax.numpy as jnp
from jax import lax

NF = 256
NT = 1024
NS = 4096
F = 16
NR = 128


def window_pair(key):
    onset = jax.random.randint(jax.random.fold_in(key, 11), (F, NR), 0, NT // 2)
    length = jax.random.randint(jax.random.fold_in(key, 12), (F, NR), NT // 8, NT // 2 + 1)
    return (onset.astype(jnp.int32), (onset + length).astype(jnp.int32))


def draw_window_onset(key, part):
    return window_pair(key)[0]


def draw_window_end(key, part):
    return window_pair(key)[1]


def level_of(stream_key, dims, split, low, top_value):
    loudness, own = 1.0, jax.random.fold_in(stream_key, 6)
    for axis_at, blocks in split:
        draws = jnp.exp(jax.random.uniform(jax.random.fold_in(own, axis_at), (blocks,), jnp.float32, low / len(split), top_value / len(split)))
        loudness = loudness * jnp.repeat(draws, dims[axis_at] // blocks).reshape([-1 if axis == axis_at else 1 for axis in range(len(dims))])
    return loudness


def normal_values(stream_key, shape, spread, bound, pieces=(), kind=jnp.bfloat16):
    factor_of = level_of(stream_key, shape, pieces, -0.22, 0.18) if pieces else 1.0
    array = jax.random.normal(stream_key, shape, jnp.float32) * spread * factor_of
    return jnp.minimum(jnp.maximum(array, -bound), bound).astype(kind)


def setup_inputs(seed: int = 0) -> dict:
    keys = jax.random.split(jax.random.key(seed), 5)
    response = normal_values(keys[0], (2, NF, NR, NS), (2 * NS) ** -0.5, 0.0625, ((1, 8), (2, 4)))
    focusing = normal_values(keys[1], (2, NF, F, NS), 1.0, 6.0, ((1, 8), (3, 4)), jnp.float32)
    window_onset = draw_window_onset(jax.random.fold_in(keys[4], 71), 0)
    window_end = draw_window_end(jax.random.fold_in(keys[4], 71), 0)
    return {"response": response, "focusing": focusing, "window_onset": window_onset, "window_end": window_end}


def make_table(base, count):
    freqs = base + jnp.arange(count, dtype=jnp.int32)
    samples = jnp.arange(NT, dtype=jnp.int32)
    phase = (freqs[:, None] * samples[None, :] % NT).astype(jnp.float32) * (2.0 * math.pi / NT)
    scale = 1.0 / math.sqrt(NF)
    return jnp.stack([jnp.cos(phase) * scale, -jnp.sin(phase) * scale])

def reference(response, focusing, window_onset, window_end):
    focus_half = focusing.astype(jnp.bfloat16)

    def one_freq(index):
        real_resp = response[0, index]
        imag_resp = response[1, index]
        real_focus = focus_half[0, index]
        imag_focus = focus_half[1, index]
        real_part = jnp.dot(real_resp, real_focus.T, preferred_element_type=jnp.float32) - jnp.dot(imag_resp, imag_focus.T, preferred_element_type=jnp.float32)
        imag_part = jnp.dot(real_resp, imag_focus.T, preferred_element_type=jnp.float32) + jnp.dot(imag_resp, real_focus.T, preferred_element_type=jnp.float32)
        return jnp.stack([real_part, imag_part])
    spectra = lax.map(one_freq, jnp.arange(NF, dtype=jnp.int32))
    table = make_table(0, NF)
    traces = jnp.einsum('kcrq,ckt->qrt', spectra, table, precision=lax.Precision.HIGHEST)
    samples = jnp.arange(NT, dtype=jnp.int32)
    keep = (samples[None, None, :] >= window_onset[:, :, None]) & (samples[None, None, :] < window_end[:, :, None])
    return jnp.where(keep, traces, jnp.float32(0.0))
```

```python
import functools
import math

import jax
import jax.numpy as jnp
import numpy as np
from jax import lax
from jax.experimental import pallas as pl
from jax.experimental.pallas import tpu as pltpu
from jax.sharding import PartitionSpec as P

NT = 1024
LANES = 128
MESH = pl.DeviceIdType.MESH


def make_table(count):
    phase = (np.arange(count)[:, None] * np.arange(NT)[None, :] % NT) * (2.0 * math.pi / NT)
    scale = 1.0 / math.sqrt(count)
    table = np.stack([np.cos(phase) * scale, -np.sin(phase) * scale], 1)
    return table.reshape(2 * count, NT).astype(np.float32)


def offloaded_groups(line, groups, rows, focal):
    if line < 4:
        return 0
    return min(groups, (line - 2) * groups * focal // (focal + rows))


def spectra_kernel(
    line, across, lent, resp_hbm, focus_hbm, out_ref,
    resp, focus, held, guest, acc, back_out, back_in, xsend, xrecv,
    resp_sem, focus_sem, send_sem, recv_sem, guest_send, guest_recv,
    back_send, back_recv, x_send, x_recv, x_local,
):
    me = lax.axis_index("recv")
    mine = lax.axis_index("freq")
    _, freqs, rows, _ = resp_hbm.shape
    focal, depth = focus_hbm.shape[2], focus_hbm.shape[3]
    groups = acc.shape[0]
    per = freqs // groups
    owned = rows // across
    kept = groups - lent
    has_left, has_right = me > 0, me < line - 1
    is_first, is_last = me == 0, me == line - 1
    left, right = jnp.maximum(me - 1, 0), jnp.minimum(me + 1, line - 1)

    def load_focus(g):
        return pltpu.make_async_copy(
            focus_hbm.at[:, pl.ds(g * per, per)], focus.at[:, pl.ds(g * per, per)], focus_sem.at[g]
        )

    def load_resp(g):
        return pltpu.make_async_copy(
            resp_hbm.at[:, pl.ds(g * per, per)], resp.at[:, pl.ds(g * per, per)], resp_sem.at[g]
        )

    for g in range(groups):
        load_focus(g).start()
    for g in range(groups):
        load_resp(g).start()

    barrier = pltpu.get_barrier_semaphore()

    @pl.when(has_left)
    def _():
        pl.semaphore_signal(barrier, inc=1, device_id={"recv": left}, device_id_type=MESH)

    @pl.when(has_right)
    def _():
        pl.semaphore_signal(barrier, inc=1, device_id={"recv": right}, device_id_type=MESH)

    for hop in range(1, across):
        other = lax.rem(mine + hop, across)
        pl.semaphore_signal(barrier, inc=1, device_id={"freq": other}, device_id_type=MESH)

    def convert(g):
        load_focus(g).wait()
        for i in range(per):
            k = g * per + i
            for part in range(2):
                held[me, k, part * focal:(part + 1) * focal, :] = focus[part, k].astype(jnp.bfloat16)

    convert(0)

    beside = has_left.astype(jnp.int32) + has_right.astype(jnp.int32)
    pl.semaphore_wait(barrier, across - 1 + beside)

    def hand_on(way, step, block, g, target):
        piece = held.at[block, pl.ds(g * per, per)]
        return pltpu.make_async_remote_copy(
            src_ref=piece, dst_ref=piece,
            send_sem=send_sem.at[way, step, g], recv_sem=recv_sem.at[block, g],
            device_id={"recv": target}, device_id_type=MESH,
        )

    def own_right(g):
        return has_right & ((me < line - 2) | (g < kept)) if lent else has_right

    def own_left(g):
        return has_left & ((me > 1) | (g < kept)) if lent else has_left

    def lend(i, target):
        columns = pl.ds(pl.multiple_of(target * depth, LANES), depth)
        return pltpu.make_async_remote_copy(
            src_ref=resp.at[:, pl.ds((kept + i) * per, per), :, columns], dst_ref=guest.at[i],
            send_sem=guest_send.at[i], recv_sem=guest_recv.at[i],
            device_id={"recv": target}, device_id_type=MESH,
        )

    def give_back(i, target):
        return pltpu.make_async_remote_copy(
            src_ref=back_out.at[i], dst_ref=back_in.at[i],
            send_sem=back_send.at[i], recv_sem=back_recv.at[i],
            device_id={"recv": target}, device_id_type=MESH,
        )

    @pl.loop(0, groups)
    def _(g):
        @pl.when(g + 1 < groups)
        def _():
            convert(g + 1)

        @pl.when(own_right(g))
        def _():
            hand_on(0, 0, me, g, right).start()

        @pl.when(own_left(g))
        def _():
            hand_on(1, 0, me, g, left).start()

    def products(left_of, block, g):
        parts = []
        for i in range(per):
            lhs = left_of(i).reshape(2 * rows, depth)
            parts.append(
                lax.dot_general(
                    lhs, held[block, g * per + i], (((1,), (1,)), ((), ())),
                    preferred_element_type=jnp.float32,
                )
            )
        return jnp.concatenate(parts, axis=1)

    def of_block(block, g):
        columns = pl.ds(pl.multiple_of(block * depth, LANES), depth)
        return products(lambda i: resp[:, g * per + i, :, columns], block, g)

    @pl.loop(0, groups)
    def _(g):
        load_resp(g).wait()

    for i in range(lent):
        @pl.when(is_first)
        def _():
            lend(i, right).start()

        @pl.when(is_last)
        def _():
            lend(i, left).start()

    @pl.loop(0, groups)
    def _(g):
        acc[g] = of_block(me, g)

    for step in range(1, line):
        from_left, from_right = me - step, me + step

        @pl.loop(0, groups)
        def _(g):
            due_left, due_right = from_left >= 0, from_right < line
            if step == 1 and lent:
                due_left = due_left & ((me < line - 1) | (g < kept))
                due_right = due_right & ((me > 0) | (g < kept))

            @pl.when(due_left)
            def _():
                block = jnp.maximum(from_left, 0)
                hand_on(0, 0, block, g, left).wait_recv()

                if step < line - 1:
                    @pl.when(has_right)
                    def _():
                        hand_on(0, step, block, g, right).start()

            @pl.when(due_right)
            def _():
                block = jnp.minimum(from_right, line - 1)
                hand_on(1, 0, block, g, right).wait_recv()

                if step < line - 1:
                    @pl.when(has_left)
                    def _():
                        hand_on(1, step, block, g, left).start()

            @pl.when(due_left)
            def _():
                acc[g] = acc[g] + of_block(jnp.maximum(from_left, 0), g)

            @pl.when(due_right)
            def _():
                acc[g] = acc[g] + of_block(jnp.minimum(from_right, line - 1), g)

    half = lax.rem(lax.broadcasted_iota(jnp.int32, (rows, LANES), 1), 2 * focal) < focal

    def combine(tile):
        real, imag = tile[:rows], tile[rows:]
        return real + jnp.where(
            half, -pltpu.roll(imag, LANES - focal, axis=1), pltpu.roll(imag, focal, axis=1)
        )

    if lent:
        for end, host in ((0, 1), (line - 1, line - 2)):
            @pl.when(me == host)
            def _():
                @pl.loop(0, lent)
                def _(i):
                    lend(i, end).wait_recv()
                    back_out[i] = combine(products(lambda n: guest[i, :, n], me, kept + i))
                    give_back(i, end).start()

    for g in range(groups):
        tile = combine(acc[g])
        if g >= kept:
            acc[g, :rows] = tile

            @pl.when(is_first | is_last)
            def _():
                give_back(g - kept, right).wait_recv()
                acc[g, :rows] = acc[g, :rows] + back_in[g - kept]

            tile = acc[g, :rows]
        for d in range(across):
            xsend[d, g * owned:(g + 1) * owned, :] = tile[d * owned:(d + 1) * owned]

    def exchange(hop):
        other = lax.rem(mine + hop, across)
        return pltpu.make_async_remote_copy(
            src_ref=xsend.at[other], dst_ref=xrecv.at[mine],
            send_sem=x_send.at[hop], recv_sem=x_recv.at[hop],
            device_id={"freq": other}, device_id_type=MESH,
        )

    for hop in range(1, across):
        exchange(hop).start()
    keep = pltpu.make_async_copy(xsend.at[mine], xrecv.at[mine], x_local)
    keep.start()

    for step in range(line - 1):
        @pl.loop(0, groups)
        def _(g):
            sent_right = own_right(g) if step == 0 else has_right & (me - step >= 0)
            sent_left = own_left(g) if step == 0 else has_left & (me + step < line)

            @pl.when(sent_right)
            def _():
                hand_on(0, step, me, g, right).wait_send()

            @pl.when(sent_left)
            def _():
                hand_on(1, step, me, g, left).wait_send()

    for i in range(lent):
        @pl.when(is_first | is_last)
        def _():
            lend(i, me).wait_send()

        @pl.when((me == 1) | (me == line - 2))
        def _():
            give_back(i, right).wait_send()

    keep.wait()
    for hop in range(1, across):
        exchange(hop).wait()
    out_ref[...] = xrecv[...]


def per_device(line, across, response, focusing, window_onset, window_end):
    _, freqs, rows, sources = response.shape
    focal, depth = focusing.shape[2], focusing.shape[3]
    per = LANES // (2 * focal)
    groups = freqs // per
    owned = rows // across
    lent = offloaded_groups(line, groups, rows, focal)
    slots = max(lent, 1)
    dma = pltpu.SemaphoreType.DMA
    moved = pl.pallas_call(
        functools.partial(spectra_kernel, line, across, lent),
        out_shape=jax.ShapeDtypeStruct((across, groups * owned, LANES), jnp.float32),
        in_specs=[pl.BlockSpec(memory_space=pl.ANY)] * 2,
        out_specs=pl.BlockSpec(memory_space=pltpu.VMEM),
        scratch_shapes=[
            pltpu.VMEM(response.shape, jnp.bfloat16),
            pltpu.VMEM(focusing.shape, jnp.float32),
            pltpu.VMEM((line, freqs, 2 * focal, depth), jnp.bfloat16),
            pltpu.VMEM((slots, 2, per, rows, depth), jnp.bfloat16),
            pltpu.VMEM((groups, 2 * rows, LANES), jnp.float32),
            pltpu.VMEM((slots, rows, LANES), jnp.float32),
            pltpu.VMEM((slots, rows, LANES), jnp.float32),
            pltpu.VMEM((across, groups * owned, LANES), jnp.float32),
            pltpu.VMEM((across, groups * owned, LANES), jnp.float32),
            dma((groups,)),
            dma((groups,)),
            dma((2, max(line - 1, 1), groups)),
            dma((line, groups)),
            dma((slots,)),
            dma((slots,)),
            dma((slots,)),
            dma((slots,)),
            dma((across,)),
            dma((across,)),
            dma,
        ],
        compiler_params=pltpu.CompilerParams(
            collective_id=0, has_side_effects=True, vmem_limit_bytes=60000 * 1024
        ),
    )(response, focusing)
    count = freqs * across
    flat = moved.reshape(across, groups, owned, per, 2, focal)
    flat = jnp.transpose(flat, (5, 2, 0, 1, 3, 4)).reshape(focal * owned, 2 * count)
    traces = jnp.dot(
        flat, make_table(count), precision=lax.Precision.HIGHEST, preferred_element_type=jnp.float32
    ).reshape(focal, owned, NT)
    samples = jnp.arange(NT, dtype=jnp.int32)
    keep = (samples[None, None, :] >= window_onset[:, :, None]) & (
        samples[None, None, :] < window_end[:, :, None]
    )
    return jnp.where(keep, traces, jnp.float32(0.0))


def solution(mesh):
    line, across = mesh.shape["recv"], mesh.shape["freq"]
    in_specs = (
        P(None, "freq", "recv", None),
        P(None, "freq", None, "recv"),
        P(None, ("recv", "freq")),
        P(None, ("recv", "freq")),
    )
    out_specs = P(None, ("recv", "freq"), None)
    return jax.shard_map(
        functools.partial(per_device, line, across),
        mesh=mesh, in_specs=in_specs, out_specs=out_specs, check_vma=False,
    )
```

```python
import functools
import math

import jax
import jax.numpy as jnp
import numpy as np
from jax import lax
from jax.experimental import pallas as pl
from jax.experimental.pallas import tpu as pltpu
from jax.sharding import PartitionSpec as P

NT = 1024
LANES = 128
MESH = pl.DeviceIdType.MESH


def make_tables(across, groups, per, room):
    freqs = groups * per
    count = across * freqs
    phase = (np.arange(count)[:, None] * np.arange(NT)[None, :] % NT) * (2.0 * math.pi / NT)
    scale = 1.0 / math.sqrt(count)
    table = np.stack([np.cos(phase) * scale, -np.sin(phase) * scale], 1)
    table = table.reshape(across, groups, per, 2, NT).transpose(2, 3, 0, 1, 4)
    early = np.zeros((per, 2, across, room, NT))
    early[:, :, :, :groups - 1] = table[:, :, :, :groups - 1]
    both = np.concatenate([early.reshape(-1, NT), table[:, :, :, groups - 1].reshape(-1, NT)])
    high = both.astype(np.float32).astype(jnp.bfloat16)
    low = (both - high.astype(np.float64)).astype(np.float32).astype(jnp.bfloat16)
    return np.stack([high, low])


def offloaded_groups(line, groups, rows, focal):
    if line < 4:
        return 0
    return min(groups, (line - 2) * groups * focal // (focal + rows))


def spectra_kernel(
    line, across, lent, resp_hbm, focus_hbm, table_hbm, out_ref,
    resp, focus, held, guest, acc, back_out, back_in, table,
    early_out, early_in, early_rows, late_out, late_in, late_rows,
    resp_sem, focus_sem, table_sem, send_sem, recv_sem, guest_send, guest_recv,
    back_send, back_recv, x_send, x_recv, x_local,
):
    me = lax.axis_index("recv")
    mine = lax.axis_index("freq")
    _, freqs, rows, _ = resp_hbm.shape
    focal, depth = focus_hbm.shape[2], focus_hbm.shape[3]
    groups = acc.shape[0]
    per = freqs // groups
    owned = rows // across
    kept = groups - lent
    has_left, has_right = me > 0, me < line - 1
    is_first, is_last = me == 0, me == line - 1
    left, right = jnp.maximum(me - 1, 0), jnp.minimum(me + 1, line - 1)

    def load_focus(g):
        return pltpu.make_async_copy(
            focus_hbm.at[:, pl.ds(g * per, per)], focus.at[:, pl.ds(g * per, per)], focus_sem.at[g]
        )

    def load_resp(g):
        return pltpu.make_async_copy(
            resp_hbm.at[:, pl.ds(g * per, per)], resp.at[:, pl.ds(g * per, per)], resp_sem.at[g]
        )

    for g in range(groups):
        load_focus(g).start()
    for g in range(groups):
        load_resp(g).start()

    load_table = pltpu.make_async_copy(table_hbm, table, table_sem)
    load_table.start()

    barrier = pltpu.get_barrier_semaphore()

    @pl.when(has_left)
    def _():
        pl.semaphore_signal(barrier, inc=1, device_id={"recv": left}, device_id_type=MESH)

    @pl.when(has_right)
    def _():
        pl.semaphore_signal(barrier, inc=1, device_id={"recv": right}, device_id_type=MESH)

    for hop in range(1, across):
        other = lax.rem(mine + hop, across)
        pl.semaphore_signal(barrier, inc=1, device_id={"freq": other}, device_id_type=MESH)

    def convert(g):
        load_focus(g).wait()
        for i in range(per):
            k = g * per + i
            for part in range(2):
                held[me, k, part * focal:(part + 1) * focal, :] = focus[part, k].astype(jnp.bfloat16)

    convert(0)

    beside = has_left.astype(jnp.int32) + has_right.astype(jnp.int32)
    pl.semaphore_wait(barrier, across - 1 + beside)

    def hand_on(way, step, block, g, target):
        piece = held.at[block, pl.ds(g * per, per)]
        return pltpu.make_async_remote_copy(
            src_ref=piece, dst_ref=piece,
            send_sem=send_sem.at[way, step, g], recv_sem=recv_sem.at[block, g],
            device_id={"recv": target}, device_id_type=MESH,
        )

    def own_right(g):
        return has_right & ((me < line - 2) | (g < kept)) if lent else has_right

    def own_left(g):
        return has_left & ((me > 1) | (g < kept)) if lent else has_left

    def lend(i, target):
        columns = pl.ds(pl.multiple_of(target * depth, LANES), depth)
        return pltpu.make_async_remote_copy(
            src_ref=resp.at[:, pl.ds((kept + i) * per, per), :, columns], dst_ref=guest.at[i],
            send_sem=guest_send.at[i], recv_sem=guest_recv.at[i],
            device_id={"recv": target}, device_id_type=MESH,
        )

    def give_back(i, target):
        return pltpu.make_async_remote_copy(
            src_ref=back_out.at[i], dst_ref=back_in.at[i],
            send_sem=back_send.at[i], recv_sem=back_recv.at[i],
            device_id={"recv": target}, device_id_type=MESH,
        )

    @pl.loop(0, groups)
    def _(g):
        @pl.when(g + 1 < groups)
        def _():
            convert(g + 1)

        @pl.when(own_right(g))
        def _():
            hand_on(0, 0, me, g, right).start()

        @pl.when(own_left(g))
        def _():
            hand_on(1, 0, me, g, left).start()

    def products(left_of, block, g):
        parts = []
        for i in range(per):
            lhs = left_of(i).reshape(2 * rows, depth)
            parts.append(
                lax.dot_general(
                    lhs, held[block, g * per + i], (((1,), (1,)), ((), ())),
                    preferred_element_type=jnp.float32,
                )
            )
        return jnp.concatenate(parts, axis=1)

    def of_block(block, g):
        columns = pl.ds(pl.multiple_of(block * depth, LANES), depth)
        return products(lambda i: resp[:, g * per + i, :, columns], block, g)

    @pl.loop(0, groups)
    def _(g):
        load_resp(g).wait()

    for i in range(lent):
        @pl.when(is_first)
        def _():
            lend(i, right).start()

        @pl.when(is_last)
        def _():
            lend(i, left).start()

    @pl.loop(0, groups)
    def _(g):
        acc[g] = of_block(me, g)

    half = lax.rem(lax.broadcasted_iota(jnp.int32, (rows, LANES), 1), 2 * focal) < focal

    def combine(tile):
        real, imag = tile[:rows], tile[rows:]
        return real + jnp.where(
            half, -pltpu.roll(imag, LANES - focal, axis=1), pltpu.roll(imag, focal, axis=1)
        )

    is_host = ((me == 1) | (me == line - 2)) if lent else False
    end = jnp.where(me == 1, 0, line - 1)
    served = min(lent, groups // 2)

    def serve(i):
        lend(i, end).wait_recv()
        back_out[i] = combine(products(lambda n: guest[i, :, n], me, kept + i))
        give_back(i, end).start()

    def visit(step, g):
        from_left, from_right = me - step, me + step
        due_left, due_right = from_left >= 0, from_right < line
        if step == 1 and lent:
            due_left = due_left & ((me < line - 1) | (g < kept))
            due_right = due_right & ((me > 0) | (g < kept))

        @pl.when(due_left)
        def _():
            block = jnp.maximum(from_left, 0)
            hand_on(0, 0, block, g, left).wait_recv()

            if step < line - 1:
                @pl.when(has_right)
                def _():
                    hand_on(0, step, block, g, right).start()

        @pl.when(due_right)
        def _():
            block = jnp.minimum(from_right, line - 1)
            hand_on(1, 0, block, g, right).wait_recv()

            if step < line - 1:
                @pl.when(has_left)
                def _():
                    hand_on(1, step, block, g, left).start()

        @pl.when(due_left)
        def _():
            acc[g] = acc[g] + of_block(jnp.maximum(from_left, 0), g)

        @pl.when(due_right)
        def _():
            acc[g] = acc[g] + of_block(jnp.minimum(from_right, line - 1), g)

        if step == line - 2 and served:
            @pl.when(is_host & (g % 2 == 1) & (g // 2 < served))
            def _():
                serve(g // 2)

    for step in range(1, line):
        @pl.loop(0, groups - 1 if step == line - 1 else groups)
        def _(g):
            visit(step, g)

    def finish(g):
        tile = combine(acc[g])
        if g < kept:
            return tile
        acc[g, :rows] = tile

        @pl.when(is_first | is_last)
        def _():
            give_back(g - kept, right).wait_recv()
            acc[g, :rows] = acc[g, :rows] + back_in[g - kept]

        return acc[g, :rows]

    def exchange(part, source, target):
        copies = []
        for hop in range(1, across):
            other = lax.rem(mine + hop, across)
            copies.append(pltpu.make_async_remote_copy(
                src_ref=source.at[other], dst_ref=target.at[mine],
                send_sem=x_send.at[part, hop], recv_sem=x_recv.at[part, hop],
                device_id={"freq": other}, device_id_type=MESH,
            ))
        copies.append(pltpu.make_async_copy(source.at[mine], target.at[mine], x_local.at[part]))
        return copies

    def transform(source, first):
        parts = []
        for m in range(2 * per):
            lanes = [source[r, :, m * focal:(m + 1) * focal] for r in range(owned)]
            parts.append(jnp.concatenate(lanes, axis=1))
        values = jnp.concatenate(parts, axis=0)
        high = values.astype(jnp.bfloat16)
        low = (values - high.astype(jnp.float32)).astype(jnp.bfloat16)
        span = slice(first, first + values.shape[0])

        def dot(a, b):
            return lax.dot_general(a, b, (((0,), (0,)), ((), ())), preferred_element_type=jnp.float32)

        return dot(high, table[0, span]) + (dot(low, table[0, span]) + dot(high, table[1, span]))

    for g in range(groups - 1):
        tile = finish(g)
        for d in range(across):
            early_out[d, g * owned:(g + 1) * owned, :] = tile[d * owned:(d + 1) * owned]
    early = exchange(0, early_out, early_in)
    for copy in early:
        copy.start()
    early_rows[...] = jnp.zeros_like(early_rows)
    load_table.wait()
    for copy in early:
        copy.wait()
    room = early_rows.shape[1] // across
    for f in range(across):
        for r in range(owned):
            early_rows[r, f * room:f * room + groups - 1, :] = early_in[
                f, pl.ds(r, groups - 1, stride=owned), :
            ]
    out_ref[...] = transform(early_rows, 0)

    @pl.when(is_host)
    def _():
        for i in range(served, lent):
            serve(i)

    visit(line - 1, groups - 1)

    tile = finish(groups - 1)
    for d in range(across):
        late_out[d] = tile[d * owned:(d + 1) * owned]
    late = exchange(1, late_out, late_in)
    for copy in late:
        copy.start()
    for copy in late:
        copy.wait()
    for f in range(across):
        for r in range(owned):
            late_rows[r, f:f + 1, :] = late_in[f, r:r + 1, :]
    out_ref[...] += transform(late_rows, 2 * per * across * room)

    for step in range(line - 1):
        @pl.loop(0, groups)
        def _(g):
            sent_right = own_right(g) if step == 0 else has_right & (me - step >= 0)
            sent_left = own_left(g) if step == 0 else has_left & (me + step < line)

            @pl.when(sent_right)
            def _():
                hand_on(0, step, me, g, right).wait_send()

            @pl.when(sent_left)
            def _():
                hand_on(1, step, me, g, left).wait_send()

    for i in range(lent):
        @pl.when(is_first | is_last)
        def _():
            lend(i, me).wait_send()

        @pl.when((me == 1) | (me == line - 2))
        def _():
            give_back(i, right).wait_send()


def per_device(line, across, response, focusing, window_onset, window_end):
    _, freqs, rows, sources = response.shape
    focal, depth = focusing.shape[2], focusing.shape[3]
    per = LANES // (2 * focal)
    groups = freqs // per
    owned = rows // across
    lent = offloaded_groups(line, groups, rows, focal)
    slots = max(lent, 1)
    room = -(-(groups - 1) // 8) * 8
    tables = make_tables(across, groups, per, room)
    dma = pltpu.SemaphoreType.DMA
    traces = pl.pallas_call(
        functools.partial(spectra_kernel, line, across, lent),
        out_shape=jax.ShapeDtypeStruct((owned * focal, NT), jnp.float32),
        in_specs=[pl.BlockSpec(memory_space=pl.ANY)] * 3,
        out_specs=pl.BlockSpec(memory_space=pltpu.VMEM),
        scratch_shapes=[
            pltpu.VMEM(response.shape, jnp.bfloat16),
            pltpu.VMEM(focusing.shape, jnp.float32),
            pltpu.VMEM((line, freqs, 2 * focal, depth), jnp.bfloat16),
            pltpu.VMEM((slots, 2, per, rows, depth), jnp.bfloat16),
            pltpu.VMEM((groups, 2 * rows, LANES), jnp.float32),
            pltpu.VMEM((slots, rows, LANES), jnp.float32),
            pltpu.VMEM((slots, rows, LANES), jnp.float32),
            pltpu.VMEM(tables.shape, jnp.bfloat16),
            pltpu.VMEM((across, (groups - 1) * owned, LANES), jnp.float32),
            pltpu.VMEM((across, (groups - 1) * owned, LANES), jnp.float32),
            pltpu.VMEM((owned, across * room, LANES), jnp.float32),
            pltpu.VMEM((across, owned, LANES), jnp.float32),
            pltpu.VMEM((across, owned, LANES), jnp.float32),
            pltpu.VMEM((owned, across, LANES), jnp.float32),
            dma((groups,)),
            dma((groups,)),
            dma,
            dma((2, max(line - 1, 1), groups)),
            dma((line, groups)),
            dma((slots,)),
            dma((slots,)),
            dma((slots,)),
            dma((slots,)),
            dma((2, across)),
            dma((2, across)),
            dma((2,)),
        ],
        compiler_params=pltpu.CompilerParams(
            collective_id=0, has_side_effects=True, vmem_limit_bytes=60000 * 1024
        ),
    )(response, focusing, tables)
    traces = jnp.transpose(traces.reshape(owned, focal, NT), (1, 0, 2))
    samples = jnp.arange(NT, dtype=jnp.int32)
    keep = (samples[None, None, :] >= window_onset[:, :, None]) & (
        samples[None, None, :] < window_end[:, :, None]
    )
    return jnp.where(keep, traces, jnp.float32(0.0))


def solution(mesh):
    line, across = mesh.shape["recv"], mesh.shape["freq"]
    in_specs = (
        P(None, "freq", "recv", None),
        P(None, "freq", None, "recv"),
        P(None, ("recv", "freq")),
        P(None, ("recv", "freq")),
    )
    out_specs = P(None, ("recv", "freq"), None)
    return jax.shard_map(
        functools.partial(per_device, line, across),
        mesh=mesh, in_specs=in_specs, out_specs=out_specs, check_vma=False,
    )
```

```python
import functools
import math

import jax
import jax.numpy as jnp
import numpy as np
from jax import lax
from jax.experimental import pallas as pl
from jax.experimental.pallas import tpu as pltpu
from jax.sharding import PartitionSpec as P

NT = 1024
LANES = 128
MESH = pl.DeviceIdType.MESH


def make_tables(across, groups, per, room):
    freqs = groups * per
    count = across * freqs
    phase = (np.arange(count)[:, None] * np.arange(NT)[None, :] % NT) * (2.0 * math.pi / NT)
    scale = 1.0 / math.sqrt(count)
    table = np.stack([np.cos(phase) * scale, -np.sin(phase) * scale], 1)
    table = table.reshape(across, groups, per, 2, NT).transpose(2, 3, 0, 1, 4)
    early = np.zeros((per, 2, across, room, NT))
    early[:, :, :, :groups - 1] = table[:, :, :, :groups - 1]
    both = np.concatenate([early.reshape(-1, NT), table[:, :, :, groups - 1].reshape(-1, NT)])
    high = both.astype(np.float32).astype(jnp.bfloat16)
    low = (both - high.astype(np.float64)).astype(np.float32).astype(jnp.bfloat16)
    return np.stack([high, low])


def offloaded_groups(line, groups, rows, focal):
    if line < 4:
        return 0
    return min(groups, (line - 2) * groups * focal // (focal + rows))


def spectra_kernel(
    line, across, lent, resp_hbm, focus_hbm, table_hbm, onset_hbm, end_hbm, out_ref,
    resp, focus, held, guest, acc, back_out, back_in, table, onset, finale, traces,
    early_out, early_in, early_rows, late_out, late_in, late_rows,
    resp_sem, focus_sem, table_sem, onset_sem, finale_sem, send_sem, recv_sem, guest_send, guest_recv,
    back_send, back_recv, x_send, x_recv, x_local,
):
    me = lax.axis_index("recv")
    mine = lax.axis_index("freq")
    _, freqs, rows, _ = resp_hbm.shape
    focal, depth = focus_hbm.shape[2], focus_hbm.shape[3]
    groups = acc.shape[0]
    per = freqs // groups
    owned = rows // across
    kept = groups - lent
    has_left, has_right = me > 0, me < line - 1
    is_first, is_last = me == 0, me == line - 1
    left, right = jnp.maximum(me - 1, 0), jnp.minimum(me + 1, line - 1)

    def load_focus(g):
        return pltpu.make_async_copy(
            focus_hbm.at[:, pl.ds(g * per, per)], focus.at[:, pl.ds(g * per, per)], focus_sem.at[g]
        )

    def load_resp(g):
        return pltpu.make_async_copy(
            resp_hbm.at[:, pl.ds(g * per, per)], resp.at[:, pl.ds(g * per, per)], resp_sem.at[g]
        )

    for g in range(groups):
        load_focus(g).start()
    for g in range(groups):
        load_resp(g).start()

    load_table = pltpu.make_async_copy(table_hbm, table, table_sem)
    load_table.start()
    load_onset = pltpu.make_async_copy(onset_hbm, onset, onset_sem)
    load_onset.start()
    load_finale = pltpu.make_async_copy(end_hbm, finale, finale_sem)
    load_finale.start()

    barrier = pltpu.get_barrier_semaphore()

    @pl.when(has_left)
    def _():
        pl.semaphore_signal(barrier, inc=1, device_id={"recv": left}, device_id_type=MESH)

    @pl.when(has_right)
    def _():
        pl.semaphore_signal(barrier, inc=1, device_id={"recv": right}, device_id_type=MESH)

    for hop in range(1, across):
        other = lax.rem(mine + hop, across)
        pl.semaphore_signal(barrier, inc=1, device_id={"freq": other}, device_id_type=MESH)

    def convert(g):
        load_focus(g).wait()
        for i in range(per):
            k = g * per + i
            for part in range(2):
                held[me, k, part * focal:(part + 1) * focal, :] = focus[part, k].astype(jnp.bfloat16)

    convert(0)

    beside = has_left.astype(jnp.int32) + has_right.astype(jnp.int32)
    pl.semaphore_wait(barrier, across - 1 + beside)

    def hand_on(way, step, block, g, target):
        piece = held.at[block, pl.ds(g * per, per)]
        return pltpu.make_async_remote_copy(
            src_ref=piece, dst_ref=piece,
            send_sem=send_sem.at[way, step, g], recv_sem=recv_sem.at[block, g],
            device_id={"recv": target}, device_id_type=MESH,
        )

    def own_right(g):
        return has_right & ((me < line - 2) | (g < kept)) if lent else has_right

    def own_left(g):
        return has_left & ((me > 1) | (g < kept)) if lent else has_left

    def lend(i, target):
        columns = pl.ds(pl.multiple_of(target * depth, LANES), depth)
        return pltpu.make_async_remote_copy(
            src_ref=resp.at[:, pl.ds((kept + i) * per, per), :, columns], dst_ref=guest.at[i],
            send_sem=guest_send.at[i], recv_sem=guest_recv.at[i],
            device_id={"recv": target}, device_id_type=MESH,
        )

    def give_back(i, target):
        return pltpu.make_async_remote_copy(
            src_ref=back_out.at[i], dst_ref=back_in.at[i],
            send_sem=back_send.at[i], recv_sem=back_recv.at[i],
            device_id={"recv": target}, device_id_type=MESH,
        )

    @pl.loop(0, groups)
    def _(g):
        @pl.when(g + 1 < groups)
        def _():
            convert(g + 1)

        @pl.when(own_right(g))
        def _():
            hand_on(0, 0, me, g, right).start()

        @pl.when(own_left(g))
        def _():
            hand_on(1, 0, me, g, left).start()

    def products(left_of, block, g):
        parts = []
        for i in range(per):
            lhs = left_of(i).reshape(2 * rows, depth)
            parts.append(
                lax.dot_general(
                    lhs, held[block, g * per + i], (((1,), (1,)), ((), ())),
                    preferred_element_type=jnp.float32,
                )
            )
        return jnp.concatenate(parts, axis=1)

    def of_block(block, g):
        columns = pl.ds(pl.multiple_of(block * depth, LANES), depth)
        return products(lambda i: resp[:, g * per + i, :, columns], block, g)

    @pl.loop(0, groups)
    def _(g):
        load_resp(g).wait()

    for i in range(lent):
        @pl.when(is_first)
        def _():
            lend(i, right).start()

        @pl.when(is_last)
        def _():
            lend(i, left).start()

    @pl.loop(0, groups)
    def _(g):
        acc[g] = of_block(me, g)

    half = lax.rem(lax.broadcasted_iota(jnp.int32, (rows, LANES), 1), 2 * focal) < focal

    def combine(tile):
        real, imag = tile[:rows], tile[rows:]
        return real + jnp.where(
            half, -pltpu.roll(imag, LANES - focal, axis=1), pltpu.roll(imag, focal, axis=1)
        )

    is_host = ((me == 1) | (me == line - 2)) if lent else False
    end = jnp.where(me == 1, 0, line - 1)
    served = min(lent, groups // 2)

    def serve(i):
        lend(i, end).wait_recv()
        back_out[i] = combine(products(lambda n: guest[i, :, n], me, kept + i))
        give_back(i, end).start()

    def visit(step, g):
        from_left, from_right = me - step, me + step
        if step == line - 2 and served:
            @pl.when(is_host & (g % 2 == 1) & (g // 2 < served))
            def _():
                serve(g // 2)

        due_left, due_right = from_left >= 0, from_right < line
        if step == 1 and lent:
            due_left = due_left & ((me < line - 1) | (g < kept))
            due_right = due_right & ((me > 0) | (g < kept))

        @pl.when(due_left)
        def _():
            block = jnp.maximum(from_left, 0)
            hand_on(0, 0, block, g, left).wait_recv()

            if step < line - 1:
                @pl.when(has_right)
                def _():
                    hand_on(0, step, block, g, right).start()

        @pl.when(due_right)
        def _():
            block = jnp.minimum(from_right, line - 1)
            hand_on(1, 0, block, g, right).wait_recv()

            if step < line - 1:
                @pl.when(has_left)
                def _():
                    hand_on(1, step, block, g, left).start()

        @pl.when(due_left)
        def _():
            acc[g] = acc[g] + of_block(jnp.maximum(from_left, 0), g)

        @pl.when(due_right)
        def _():
            acc[g] = acc[g] + of_block(jnp.minimum(from_right, line - 1), g)

    for step in range(1, line):
        @pl.loop(0, groups - 1 if step == line - 1 else groups)
        def _(g):
            visit(step, g)

    def finish(g):
        tile = combine(acc[g])
        if g < kept:
            return tile
        acc[g, :rows] = tile

        @pl.when(is_first | is_last)
        def _():
            give_back(g - kept, right).wait_recv()
            acc[g, :rows] = acc[g, :rows] + back_in[g - kept]

        return acc[g, :rows]

    def exchange(part, source, target):
        copies = []
        for hop in range(1, across):
            other = lax.rem(mine + hop, across)
            copies.append(pltpu.make_async_remote_copy(
                src_ref=source.at[other], dst_ref=target.at[mine],
                send_sem=x_send.at[part, hop], recv_sem=x_recv.at[part, hop],
                device_id={"freq": other}, device_id_type=MESH,
            ))
        copies.append(pltpu.make_async_copy(source.at[mine], target.at[mine], x_local.at[part]))
        return copies

    def transform(source, first):
        parts = []
        for m in range(2 * per):
            lanes = [source[r, :, m * focal:(m + 1) * focal] for r in range(owned)]
            parts.append(jnp.concatenate(lanes, axis=1))
        values = jnp.concatenate(parts, axis=0)
        high = values.astype(jnp.bfloat16)
        low = (values - high.astype(jnp.float32)).astype(jnp.bfloat16)
        span = slice(first, first + values.shape[0])

        def dot(a, b):
            return lax.dot_general(a, b, (((0,), (0,)), ((), ())), preferred_element_type=jnp.float32)

        return dot(high, table[0, span]) + (dot(low, table[0, span]) + dot(high, table[1, span]))

    for g in range(groups - 1):
        tile = finish(g)
        for d in range(across):
            early_out[d, g * owned:(g + 1) * owned, :] = tile[d * owned:(d + 1) * owned]
    early = exchange(0, early_out, early_in)
    for copy in early:
        copy.start()
    early_rows[...] = jnp.zeros_like(early_rows)
    load_table.wait()
    load_onset.wait()
    load_finale.wait()
    for copy in early:
        copy.wait()
    room = early_rows.shape[1] // across
    for f in range(across):
        for r in range(owned):
            early_rows[r, f * room:f * room + groups - 1, :] = early_in[
                f, pl.ds(r, groups - 1, stride=owned), :
            ]
    traces[...] = transform(early_rows, 0)

    @pl.when(is_host)
    def _():
        for i in range(served, lent):
            serve(i)

    visit(line - 1, groups - 1)

    tile = finish(groups - 1)
    for d in range(across):
        late_out[d] = tile[d * owned:(d + 1) * owned]
    late = exchange(1, late_out, late_in)
    for copy in late:
        copy.start()
    for copy in late:
        copy.wait()
    for f in range(across):
        for r in range(owned):
            late_rows[r, f:f + 1, :] = late_in[f, r:r + 1, :]
    total = traces[...] + transform(late_rows, 2 * per * across * room)
    samples = lax.broadcasted_iota(jnp.int32, (focal, NT), 1)
    starts, ends = jnp.transpose(onset[...]), jnp.transpose(finale[...])
    for r in range(owned):
        inside = (samples >= starts[:, r:r + 1]) & (samples < ends[:, r:r + 1])
        windowed = jnp.where(inside, total[r * focal:(r + 1) * focal], 0.0)
        for q in range(focal):
            out_ref[q, r:r + 1, :] = windowed[q:q + 1]

    for step in range(line - 1):
        @pl.loop(0, groups)
        def _(g):
            sent_right = own_right(g) if step == 0 else has_right & (me - step >= 0)
            sent_left = own_left(g) if step == 0 else has_left & (me + step < line)

            @pl.when(sent_right)
            def _():
                hand_on(0, step, me, g, right).wait_send()

            @pl.when(sent_left)
            def _():
                hand_on(1, step, me, g, left).wait_send()

    for i in range(lent):
        @pl.when(is_first | is_last)
        def _():
            lend(i, me).wait_send()

        @pl.when((me == 1) | (me == line - 2))
        def _():
            give_back(i, right).wait_send()


def per_device(line, across, response, focusing, window_onset, window_end):
    _, freqs, rows, sources = response.shape
    focal, depth = focusing.shape[2], focusing.shape[3]
    per = LANES // (2 * focal)
    groups = freqs // per
    owned = rows // across
    lent = offloaded_groups(line, groups, rows, focal)
    slots = max(lent, 1)
    room = -(-(groups - 1) // 8) * 8
    tables = make_tables(across, groups, per, room)
    dma = pltpu.SemaphoreType.DMA
    return pl.pallas_call(
        functools.partial(spectra_kernel, line, across, lent),
        out_shape=jax.ShapeDtypeStruct((focal, owned, NT), jnp.float32),
        in_specs=[pl.BlockSpec(memory_space=pl.ANY)] * 5,
        out_specs=pl.BlockSpec(memory_space=pltpu.VMEM),
        scratch_shapes=[
            pltpu.VMEM(response.shape, jnp.bfloat16),
            pltpu.VMEM(focusing.shape, jnp.float32),
            pltpu.VMEM((line, freqs, 2 * focal, depth), jnp.bfloat16),
            pltpu.VMEM((slots, 2, per, rows, depth), jnp.bfloat16),
            pltpu.VMEM((groups, 2 * rows, LANES), jnp.float32),
            pltpu.VMEM((slots, rows, LANES), jnp.float32),
            pltpu.VMEM((slots, rows, LANES), jnp.float32),
            pltpu.VMEM(tables.shape, jnp.bfloat16),
            pltpu.VMEM((owned, focal), jnp.int32),
            pltpu.VMEM((owned, focal), jnp.int32),
            pltpu.VMEM((owned * focal, NT), jnp.float32),
            pltpu.VMEM((across, (groups - 1) * owned, LANES), jnp.float32),
            pltpu.VMEM((across, (groups - 1) * owned, LANES), jnp.float32),
            pltpu.VMEM((owned, across * room, LANES), jnp.float32),
            pltpu.VMEM((across, owned, LANES), jnp.float32),
            pltpu.VMEM((across, owned, LANES), jnp.float32),
            pltpu.VMEM((owned, across, LANES), jnp.float32),
            dma((groups,)),
            dma((groups,)),
            dma,
            dma,
            dma,
            dma((2, max(line - 1, 1), groups)),
            dma((line, groups)),
            dma((slots,)),
            dma((slots,)),
            dma((slots,)),
            dma((slots,)),
            dma((2, across)),
            dma((2, across)),
            dma((2,)),
        ],
        compiler_params=pltpu.CompilerParams(
            collective_id=0, has_side_effects=True, vmem_limit_bytes=60000 * 1024
        ),
    )(response, focusing, tables, window_onset.T, window_end.T)


def solution(mesh):
    line, across = mesh.shape["recv"], mesh.shape["freq"]
    in_specs = (
        P(None, "freq", "recv", None),
        P(None, "freq", None, "recv"),
        P(None, ("recv", "freq")),
        P(None, ("recv", "freq")),
    )
    out_specs = P(None, ("recv", "freq"), None)
    return jax.shard_map(
        functools.partial(per_device, line, across),
        mesh=mesh, in_specs=in_specs, out_specs=out_specs, check_vma=False,
    )
```

```python
import functools
import math

import jax
import jax.numpy as jnp
import numpy as np
from jax import lax
from jax.experimental import pallas as pl
from jax.experimental.pallas import tpu as pltpu
from jax.sharding import PartitionSpec as P

NT = 1024
LANES = 128
MESH = pl.DeviceIdType.MESH


def make_tables(across, groups, per, room):
    freqs = groups * per
    count = across * freqs
    phase = (np.arange(count)[:, None] * np.arange(NT)[None, :] % NT) * (2.0 * math.pi / NT)
    scale = 1.0 / math.sqrt(count)
    table = np.stack([np.cos(phase) * scale, -np.sin(phase) * scale], 1)
    table = table.reshape(across, groups, per, 2, NT).transpose(2, 3, 0, 1, 4)
    early = np.zeros((per, 2, across, room, NT))
    early[:, :, :, :groups - 1] = table[:, :, :, :groups - 1]
    both = np.concatenate([early.reshape(-1, NT), table[:, :, :, groups - 1].reshape(-1, NT)])
    high = both.astype(np.float32).astype(jnp.bfloat16)
    low = (both - high.astype(np.float64)).astype(np.float32).astype(jnp.bfloat16)
    return np.stack([high, low])


def lent_freqs(line, freqs, rows, focal):
    if line < 4:
        return 0
    return min(freqs, (line - 2) * freqs * focal // (focal + rows))


def spectra_kernel(
    line, across, lent, extra, resp_hbm, focus_hbm, table_hbm, onset_hbm, end_hbm, out_ref,
    resp, focus, held, guest, acc, back_out, back_in, table, onset, finale, traces,
    early_out, early_in, early_rows, late_out, late_in, late_rows,
    resp_sem, focus_sem, table_sem, onset_sem, finale_sem, send_sem, recv_sem, guest_send, guest_recv,
    back_send, back_recv, x_send, x_recv, x_local,
):
    me = lax.axis_index("recv")
    mine = lax.axis_index("freq")
    _, freqs, rows, _ = resp_hbm.shape
    focal, depth = focus_hbm.shape[2], focus_hbm.shape[3]
    groups = acc.shape[0]
    per = freqs // groups
    owned = rows // across
    kept = groups - lent
    whole = kept - 1 if extra else kept
    rest = per - extra
    has_left, has_right = me > 0, me < line - 1
    is_first, is_last = me == 0, me == line - 1
    left, right = jnp.maximum(me - 1, 0), jnp.minimum(me + 1, line - 1)

    def load_focus(g):
        return pltpu.make_async_copy(
            focus_hbm.at[:, pl.ds(g * per, per)], focus.at[:, pl.ds(g * per, per)], focus_sem.at[g]
        )

    def load_resp(g):
        return pltpu.make_async_copy(
            resp_hbm.at[:, pl.ds(g * per, per)], resp.at[:, pl.ds(g * per, per)], resp_sem.at[g]
        )

    for g in range(groups):
        load_focus(g).start()
    for g in range(groups):
        load_resp(g).start()

    load_table = pltpu.make_async_copy(table_hbm, table, table_sem)
    load_table.start()
    load_onset = pltpu.make_async_copy(onset_hbm, onset, onset_sem)
    load_onset.start()
    load_finale = pltpu.make_async_copy(end_hbm, finale, finale_sem)
    load_finale.start()

    barrier = pltpu.get_barrier_semaphore()

    @pl.when(has_left)
    def _():
        pl.semaphore_signal(barrier, inc=1, device_id={"recv": left}, device_id_type=MESH)

    @pl.when(has_right)
    def _():
        pl.semaphore_signal(barrier, inc=1, device_id={"recv": right}, device_id_type=MESH)

    for hop in range(1, across):
        other = lax.rem(mine + hop, across)
        pl.semaphore_signal(barrier, inc=1, device_id={"freq": other}, device_id_type=MESH)

    def convert(g):
        load_focus(g).wait()
        for i in range(per):
            k = g * per + i
            for part in range(2):
                held[me, k, part * focal:(part + 1) * focal, :] = focus[part, k].astype(jnp.bfloat16)

    convert(0)

    beside = has_left.astype(jnp.int32) + has_right.astype(jnp.int32)
    pl.semaphore_wait(barrier, across - 1 + beside)

    def hand_on(way, step, block, g, target):
        piece = held.at[block, pl.ds(g * per, per)]
        return pltpu.make_async_remote_copy(
            src_ref=piece, dst_ref=piece,
            send_sem=send_sem.at[way, step, g], recv_sem=recv_sem.at[block, g],
            device_id={"recv": target}, device_id_type=MESH,
        )

    def hand_part(way, block, target):
        piece = held.at[block, pl.ds(whole * per, rest)]
        return pltpu.make_async_remote_copy(
            src_ref=piece, dst_ref=piece,
            send_sem=send_sem.at[way, 0, whole], recv_sem=recv_sem.at[block, whole],
            device_id={"recv": target}, device_id_type=MESH,
        )

    def own_right(g):
        return has_right & ((me < line - 2) | (g < whole)) if lent + extra else has_right

    def own_left(g):
        return has_left & ((me > 1) | (g < whole)) if lent + extra else has_left

    def lend(i, target):
        columns = pl.ds(pl.multiple_of(target * depth, LANES), depth)
        return pltpu.make_async_remote_copy(
            src_ref=resp.at[:, pl.ds((kept + i) * per, per), :, columns], dst_ref=guest.at[i],
            send_sem=guest_send.at[i], recv_sem=guest_recv.at[i],
            device_id={"recv": target}, device_id_type=MESH,
        )

    def lend_part(target):
        columns = pl.ds(pl.multiple_of(target * depth, LANES), depth)
        return pltpu.make_async_remote_copy(
            src_ref=resp.at[:, pl.ds(whole * per + rest, extra), :, columns],
            dst_ref=guest.at[lent, :, pl.ds(0, extra)],
            send_sem=guest_send.at[lent], recv_sem=guest_recv.at[lent],
            device_id={"recv": target}, device_id_type=MESH,
        )

    def give_back(i, target):
        return pltpu.make_async_remote_copy(
            src_ref=back_out.at[i], dst_ref=back_in.at[i],
            send_sem=back_send.at[i], recv_sem=back_recv.at[i],
            device_id={"recv": target}, device_id_type=MESH,
        )

    @pl.loop(0, groups)
    def _(g):
        @pl.when(g + 1 < groups)
        def _():
            convert(g + 1)

        @pl.when(own_right(g))
        def _():
            hand_on(0, 0, me, g, right).start()

        @pl.when(own_left(g))
        def _():
            hand_on(1, 0, me, g, left).start()

    if extra:
        @pl.when(me == line - 2)
        def _():
            hand_part(0, me, right).start()

        @pl.when(me == 1)
        def _():
            hand_part(1, me, left).start()

    def products(left_of, block, g, first=0, last=per):
        parts = []
        for i in range(per):
            if not first <= i < last:
                parts.append(jnp.zeros((2 * rows, 2 * focal), jnp.float32))
                continue
            lhs = left_of(i).reshape(2 * rows, depth)
            parts.append(
                lax.dot_general(
                    lhs, held[block, g * per + i], (((1,), (1,)), ((), ())),
                    preferred_element_type=jnp.float32,
                )
            )
        return jnp.concatenate(parts, axis=1)

    def of_block(block, g, last=per):
        columns = pl.ds(pl.multiple_of(block * depth, LANES), depth)
        return products(lambda i: resp[:, g * per + i, :, columns], block, g, 0, last)

    @pl.loop(0, groups)
    def _(g):
        load_resp(g).wait()

    if extra:
        @pl.when(is_first)
        def _():
            lend_part(right).start()

        @pl.when(is_last)
        def _():
            lend_part(left).start()

    for i in range(lent):
        @pl.when(is_first)
        def _():
            lend(i, right).start()

        @pl.when(is_last)
        def _():
            lend(i, left).start()

    @pl.loop(0, groups)
    def _(g):
        acc[g] = of_block(me, g)

    half = lax.rem(lax.broadcasted_iota(jnp.int32, (rows, LANES), 1), 2 * focal) < focal

    def combine(tile):
        real, imag = tile[:rows], tile[rows:]
        return real + jnp.where(
            half, -pltpu.roll(imag, LANES - focal, axis=1), pltpu.roll(imag, focal, axis=1)
        )

    is_host = ((me == 1) | (me == line - 2)) if lent + extra else False
    end = jnp.where(me == 1, 0, line - 1)
    served = min(lent, groups // 2)

    def serve(i):
        lend(i, end).wait_recv()
        back_out[i] = combine(products(lambda n: guest[i, :, n], me, kept + i))
        give_back(i, end).start()

    def visit(step, g):
        from_left, from_right = me - step, me + step
        if step == line - 2 and extra:
            @pl.when(is_host & (g == 0))
            def _():
                lend_part(end).wait_recv()
                tile = products(lambda n: guest[lent, :, n - rest], me, whole, rest)
                back_out[lent] = combine(tile)
                give_back(lent, end).start()

        if step == line - 2 and served:
            @pl.when(is_host & (g > 0) & (g % 2 == 0) & (g // 2 - 1 < min(served, groups // 2 - 1)))
            def _():
                serve(g // 2 - 1)

            if served == groups // 2:
                @pl.when(is_host & (g == groups - 1))
                def _():
                    serve(served - 1)

        due_left, due_right = from_left >= 0, from_right < line
        if step == 1 and lent + extra:
            due_left = due_left & ((me < line - 1) | (g < whole))
            due_right = due_right & ((me > 0) | (g < whole))

        @pl.when(due_left)
        def _():
            block = jnp.maximum(from_left, 0)
            hand_on(0, 0, block, g, left).wait_recv()

            if step < line - 1:
                @pl.when(has_right)
                def _():
                    hand_on(0, step, block, g, right).start()

        @pl.when(due_right)
        def _():
            block = jnp.minimum(from_right, line - 1)
            hand_on(1, 0, block, g, right).wait_recv()

            if step < line - 1:
                @pl.when(has_left)
                def _():
                    hand_on(1, step, block, g, left).start()

        @pl.when(due_left)
        def _():
            acc[g] = acc[g] + of_block(jnp.maximum(from_left, 0), g)

        @pl.when(due_right)
        def _():
            acc[g] = acc[g] + of_block(jnp.minimum(from_right, line - 1), g)

    for step in range(1, line):
        @pl.loop(0, groups - 1 if step == line - 1 else groups)
        def _(g):
            visit(step, g)

        if step == 1 and extra:
            for at_end, block, way, beside in ((is_first, 1, 1, right), (is_last, line - 2, 0, left)):
                @pl.when(at_end)
                def _():
                    hand_part(way, block, beside).wait_recv()
                    acc[whole] = acc[whole] + of_block(block, whole, rest)

    def finish(g):
        tile = combine(acc[g])
        if g < whole:
            return tile
        slot = lent if g < kept else g - kept
        acc[g, :rows] = tile

        @pl.when(is_first | is_last)
        def _():
            give_back(slot, right).wait_recv()
            acc[g, :rows] = acc[g, :rows] + back_in[slot]

        return acc[g, :rows]

    def exchange(part, source, target):
        copies = []
        for hop in range(1, across):
            other = lax.rem(mine + hop, across)
            copies.append(pltpu.make_async_remote_copy(
                src_ref=source.at[other], dst_ref=target.at[mine],
                send_sem=x_send.at[part, hop], recv_sem=x_recv.at[part, hop],
                device_id={"freq": other}, device_id_type=MESH,
            ))
        copies.append(pltpu.make_async_copy(source.at[mine], target.at[mine], x_local.at[part]))
        return copies

    def transform(source, first):
        parts = []
        for m in range(2 * per):
            lanes = [source[r, :, m * focal:(m + 1) * focal] for r in range(owned)]
            parts.append(jnp.concatenate(lanes, axis=1))
        values = jnp.concatenate(parts, axis=0)
        high = values.astype(jnp.bfloat16)
        low = (values - high.astype(jnp.float32)).astype(jnp.bfloat16)
        span = slice(first, first + values.shape[0])

        def dot(a, b):
            return lax.dot_general(a, b, (((0,), (0,)), ((), ())), preferred_element_type=jnp.float32)

        return dot(high, table[0, span]) + (dot(low, table[0, span]) + dot(high, table[1, span]))

    for g in range(groups - 1):
        tile = finish(g)
        for d in range(across):
            early_out[d, g * owned:(g + 1) * owned, :] = tile[d * owned:(d + 1) * owned]
    early = exchange(0, early_out, early_in)
    for copy in early:
        copy.start()
    early_rows[...] = jnp.zeros_like(early_rows)
    load_table.wait()
    load_onset.wait()
    load_finale.wait()
    for copy in early:
        copy.wait()
    room = early_rows.shape[1] // across
    for f in range(across):
        for r in range(owned):
            early_rows[r, f * room:f * room + groups - 1, :] = early_in[
                f, pl.ds(r, groups - 1, stride=owned), :
            ]
    traces[...] = transform(early_rows, 0)

    @pl.when(is_host)
    def _():
        for i in range(served, lent):
            serve(i)

    visit(line - 1, groups - 1)

    tile = finish(groups - 1)
    for d in range(across):
        late_out[d] = tile[d * owned:(d + 1) * owned]
    late = exchange(1, late_out, late_in)
    for copy in late:
        copy.start()
    for copy in late:
        copy.wait()
    for f in range(across):
        for r in range(owned):
            late_rows[r, f:f + 1, :] = late_in[f, r:r + 1, :]
    total = traces[...] + transform(late_rows, 2 * per * across * room)
    samples = lax.broadcasted_iota(jnp.int32, (focal, NT), 1)
    starts, ends = jnp.transpose(onset[...]), jnp.transpose(finale[...])
    for r in range(owned):
        inside = (samples >= starts[:, r:r + 1]) & (samples < ends[:, r:r + 1])
        windowed = jnp.where(inside, total[r * focal:(r + 1) * focal], 0.0)
        for q in range(focal):
            out_ref[q, r:r + 1, :] = windowed[q:q + 1]

    for step in range(line - 1):
        @pl.loop(0, groups)
        def _(g):
            sent_right = own_right(g) if step == 0 else has_right & (me - step >= 0)
            sent_left = own_left(g) if step == 0 else has_left & (me + step < line)

            @pl.when(sent_right)
            def _():
                hand_on(0, step, me, g, right).wait_send()

            @pl.when(sent_left)
            def _():
                hand_on(1, step, me, g, left).wait_send()

    if extra:
        @pl.when(me == line - 2)
        def _():
            hand_part(0, me, right).wait_send()

        @pl.when(me == 1)
        def _():
            hand_part(1, me, left).wait_send()

        @pl.when(is_first | is_last)
        def _():
            lend_part(me).wait_send()

        @pl.when((me == 1) | (me == line - 2))
        def _():
            give_back(lent, right).wait_send()

    for i in range(lent):
        @pl.when(is_first | is_last)
        def _():
            lend(i, me).wait_send()

        @pl.when((me == 1) | (me == line - 2))
        def _():
            give_back(i, right).wait_send()


def per_device(line, across, response, focusing, window_onset, window_end):
    _, freqs, rows, sources = response.shape
    focal, depth = focusing.shape[2], focusing.shape[3]
    per = LANES // (2 * focal)
    groups = freqs // per
    owned = rows // across
    lent, extra = divmod(lent_freqs(line, freqs, rows, focal), per)
    slots = lent + 1
    room = -(-(groups - 1) // 8) * 8
    tables = make_tables(across, groups, per, room)
    dma = pltpu.SemaphoreType.DMA
    return pl.pallas_call(
        functools.partial(spectra_kernel, line, across, lent, extra),
        out_shape=pltpu.VMEM((focal, owned, NT), jnp.float32),
        in_specs=[pl.BlockSpec(memory_space=pl.ANY)] * 5,
        out_specs=pl.BlockSpec(memory_space=pltpu.VMEM),
        scratch_shapes=[
            pltpu.VMEM(response.shape, jnp.bfloat16),
            pltpu.VMEM(focusing.shape, jnp.float32),
            pltpu.VMEM((line, freqs, 2 * focal, depth), jnp.bfloat16),
            pltpu.VMEM((slots, 2, per, rows, depth), jnp.bfloat16),
            pltpu.VMEM((groups, 2 * rows, LANES), jnp.float32),
            pltpu.VMEM((slots, rows, LANES), jnp.float32),
            pltpu.VMEM((slots, rows, LANES), jnp.float32),
            pltpu.VMEM(tables.shape, jnp.bfloat16),
            pltpu.VMEM((owned, focal), jnp.int32),
            pltpu.VMEM((owned, focal), jnp.int32),
            pltpu.VMEM((owned * focal, NT), jnp.float32),
            pltpu.VMEM((across, (groups - 1) * owned, LANES), jnp.float32),
            pltpu.VMEM((across, (groups - 1) * owned, LANES), jnp.float32),
            pltpu.VMEM((owned, across * room, LANES), jnp.float32),
            pltpu.VMEM((across, owned, LANES), jnp.float32),
            pltpu.VMEM((across, owned, LANES), jnp.float32),
            pltpu.VMEM((owned, across, LANES), jnp.float32),
            dma((groups,)),
            dma((groups,)),
            dma,
            dma,
            dma,
            dma((2, max(line - 1, 1), groups)),
            dma((line, groups)),
            dma((slots,)),
            dma((slots,)),
            dma((slots,)),
            dma((slots,)),
            dma((2, across)),
            dma((2, across)),
            dma((2,)),
        ],
        compiler_params=pltpu.CompilerParams(
            collective_id=0, has_side_effects=True, vmem_limit_bytes=60000 * 1024
        ),
    )(response, focusing, tables, window_onset.T, window_end.T)


def solution(mesh):
    line, across = mesh.shape["recv"], mesh.shape["freq"]
    in_specs = (
        P(None, "freq", "recv", None),
        P(None, "freq", None, "recv"),
        P(None, ("recv", "freq")),
        P(None, ("recv", "freq")),
    )
    out_specs = P(None, ("recv", "freq"), None)
    return jax.shard_map(
        functools.partial(per_device, line, across),
        mesh=mesh, in_specs=in_specs, out_specs=out_specs, check_vma=False,
    )
```

```python
import functools
import math

import jax
import jax.numpy as jnp
import numpy as np
from jax import lax
from jax.experimental import pallas as pl
from jax.experimental.pallas import tpu as pltpu
from jax.sharding import PartitionSpec as P

NT = 1024
LANES = 128
MESH = pl.DeviceIdType.MESH


def make_tables(across, groups, per, room):
    freqs = groups * per
    count = across * freqs
    phase = (np.arange(count)[:, None] * np.arange(NT)[None, :] % NT) * (2.0 * math.pi / NT)
    scale = 1.0 / math.sqrt(count)
    table = np.stack([np.cos(phase) * scale, -np.sin(phase) * scale], 1)
    table = table.reshape(across, groups, per, 2, NT).transpose(2, 3, 0, 1, 4)
    early = np.zeros((per, 2, across, room, NT))
    early[:, :, :, :groups - 1] = table[:, :, :, :groups - 1]
    both = np.concatenate([early.reshape(-1, NT), table[:, :, :, groups - 1].reshape(-1, NT)])
    high = both.astype(np.float32).astype(jnp.bfloat16)
    low = (both - high.astype(np.float64)).astype(np.float32).astype(jnp.bfloat16)
    return np.stack([high, low])


def lent_freqs(line, freqs, rows, focal):
    if line < 4:
        return 0
    return min(freqs, (line - 2) * freqs * focal // (focal + rows))


def spectra_kernel(
    line, across, lent, extra, resp_hbm, focus_hbm, table_hbm, onset_hbm, end_hbm, out_ref,
    resp, focus, held, guest, acc, back_out, back_in, table, onset, finale, traces,
    early_out, early_in, early_rows, late_out, late_in, late_rows,
    resp_sem, focus_sem, table_sem, onset_sem, finale_sem, send_sem, recv_sem, guest_send, guest_recv,
    back_send, back_recv, x_send, x_recv, x_local,
):
    me = lax.axis_index("recv")
    mine = lax.axis_index("freq")
    _, freqs, rows, _ = resp_hbm.shape
    focal, depth = focus_hbm.shape[2], focus_hbm.shape[3]
    groups = acc.shape[0]
    per = freqs // groups
    owned = rows // across
    kept = groups - lent
    whole = kept - 1 if extra else kept
    rest = per - extra
    has_left, has_right = me > 0, me < line - 1
    is_first, is_last = me == 0, me == line - 1
    left, right = jnp.maximum(me - 1, 0), jnp.minimum(me + 1, line - 1)

    def load_focus(g):
        return pltpu.make_async_copy(
            focus_hbm.at[:, pl.ds(g * per, per)], focus.at[:, pl.ds(g * per, per)], focus_sem.at[g]
        )

    def load_resp(g):
        return pltpu.make_async_copy(
            resp_hbm.at[:, pl.ds(g * per, per)], resp.at[:, pl.ds(g * per, per)], resp_sem.at[g]
        )

    barrier = pltpu.get_barrier_semaphore()

    @pl.when(has_left)
    def _():
        pl.semaphore_signal(barrier, inc=1, device_id={"recv": left}, device_id_type=MESH)

    @pl.when(has_right)
    def _():
        pl.semaphore_signal(barrier, inc=1, device_id={"recv": right}, device_id_type=MESH)

    for hop in range(1, across):
        other = lax.rem(mine + hop, across)
        pl.semaphore_signal(barrier, inc=1, device_id={"freq": other}, device_id_type=MESH)

    for g in range(groups):
        load_focus(g).start()
    for g in range(groups):
        load_resp(g).start()

    load_table = pltpu.make_async_copy(table_hbm, table, table_sem)
    load_table.start()
    load_onset = pltpu.make_async_copy(onset_hbm, onset, onset_sem)
    load_onset.start()
    load_finale = pltpu.make_async_copy(end_hbm, finale, finale_sem)
    load_finale.start()

    def convert(g):
        load_focus(g).wait()
        for i in range(per):
            k = g * per + i
            for part in range(2):
                held[me, k, part * focal:(part + 1) * focal, :] = focus[part, k].astype(jnp.bfloat16)

    for g in range(min(2, groups)):
        convert(g)

    beside = has_left.astype(jnp.int32) + has_right.astype(jnp.int32)
    pl.semaphore_wait(barrier, across - 1 + beside)

    def hand_on(way, step, block, g, target):
        piece = held.at[block, pl.ds(g * per, per)]
        return pltpu.make_async_remote_copy(
            src_ref=piece, dst_ref=piece,
            send_sem=send_sem.at[way, step, g], recv_sem=recv_sem.at[block, g],
            device_id={"recv": target}, device_id_type=MESH,
        )

    def hand_part(way, block, target):
        piece = held.at[block, pl.ds(whole * per, rest)]
        return pltpu.make_async_remote_copy(
            src_ref=piece, dst_ref=piece,
            send_sem=send_sem.at[way, 0, whole], recv_sem=recv_sem.at[block, whole],
            device_id={"recv": target}, device_id_type=MESH,
        )

    def own_right(g):
        return has_right & ((me < line - 2) | (g < whole)) if lent + extra else has_right

    def own_left(g):
        return has_left & ((me > 1) | (g < whole)) if lent + extra else has_left

    def lend(i, target):
        columns = pl.ds(pl.multiple_of(target * depth, LANES), depth)
        return pltpu.make_async_remote_copy(
            src_ref=resp.at[:, pl.ds((kept + i) * per, per), :, columns], dst_ref=guest.at[i],
            send_sem=guest_send.at[i], recv_sem=guest_recv.at[i],
            device_id={"recv": target}, device_id_type=MESH,
        )

    def lend_part(target):
        columns = pl.ds(pl.multiple_of(target * depth, LANES), depth)
        return pltpu.make_async_remote_copy(
            src_ref=resp.at[:, pl.ds(whole * per + rest, extra), :, columns],
            dst_ref=guest.at[lent, :, pl.ds(0, extra)],
            send_sem=guest_send.at[lent], recv_sem=guest_recv.at[lent],
            device_id={"recv": target}, device_id_type=MESH,
        )

    def give_back(i, target):
        return pltpu.make_async_remote_copy(
            src_ref=back_out.at[i], dst_ref=back_in.at[i],
            send_sem=back_send.at[i], recv_sem=back_recv.at[i],
            device_id={"recv": target}, device_id_type=MESH,
        )

    @pl.loop(0, groups)
    def _(g):
        @pl.when(own_right(g))
        def _():
            hand_on(0, 0, me, g, right).start()

        @pl.when(own_left(g))
        def _():
            hand_on(1, 0, me, g, left).start()

        @pl.when(g + 2 < groups)
        def _():
            convert(g + 2)

    if extra:
        @pl.when(me == line - 2)
        def _():
            hand_part(0, me, right).start()

        @pl.when(me == 1)
        def _():
            hand_part(1, me, left).start()

    def products(left_of, block, g, first=0, last=per):
        parts = []
        for i in range(per):
            if not first <= i < last:
                parts.append(jnp.zeros((2 * rows, 2 * focal), jnp.float32))
                continue
            lhs = left_of(i).reshape(2 * rows, depth)
            parts.append(
                lax.dot_general(
                    lhs, held[block, g * per + i], (((1,), (1,)), ((), ())),
                    preferred_element_type=jnp.float32,
                )
            )
        return jnp.concatenate(parts, axis=1)

    def of_block(block, g, last=per):
        columns = pl.ds(pl.multiple_of(block * depth, LANES), depth)
        return products(lambda i: resp[:, g * per + i, :, columns], block, g, 0, last)

    @pl.loop(0, groups)
    def _(g):
        load_resp(g).wait()

    if extra:
        @pl.when(is_first)
        def _():
            lend_part(right).start()

        @pl.when(is_last)
        def _():
            lend_part(left).start()

    for i in range(lent):
        @pl.when(is_first)
        def _():
            lend(i, right).start()

        @pl.when(is_last)
        def _():
            lend(i, left).start()

    @pl.loop(0, groups)
    def _(g):
        acc[g] = of_block(me, g)

    half = lax.rem(lax.broadcasted_iota(jnp.int32, (rows, LANES), 1), 2 * focal) < focal

    def combine(tile):
        real, imag = tile[:rows], tile[rows:]
        return real + jnp.where(
            half, -pltpu.roll(imag, LANES - focal, axis=1), pltpu.roll(imag, focal, axis=1)
        )

    is_host = ((me == 1) | (me == line - 2)) if lent + extra else False
    end = jnp.where(me == 1, 0, line - 1)
    served = min(lent, groups // 2)

    def serve(i):
        lend(i, end).wait_recv()
        back_out[i] = combine(products(lambda n: guest[i, :, n], me, kept + i))
        give_back(i, end).start()

    def visit(step, g):
        from_left, from_right = me - step, me + step
        if step == line - 2 and extra:
            @pl.when(is_host & (g == 0))
            def _():
                lend_part(end).wait_recv()
                tile = products(lambda n: guest[lent, :, n - rest], me, whole, rest)
                back_out[lent] = combine(tile)
                give_back(lent, end).start()

        if step == line - 2 and served:
            @pl.when(is_host & (g > 0) & (g % 2 == 0) & (g // 2 - 1 < min(served, groups // 2 - 1)))
            def _():
                serve(g // 2 - 1)

            if served == groups // 2:
                @pl.when(is_host & (g == groups - 1))
                def _():
                    serve(served - 1)

        due_left, due_right = from_left >= 0, from_right < line
        if step == 1 and lent + extra:
            due_left = due_left & ((me < line - 1) | (g < whole))
            due_right = due_right & ((me > 0) | (g < whole))

        @pl.when(due_left)
        def _():
            block = jnp.maximum(from_left, 0)
            hand_on(0, 0, block, g, left).wait_recv()

            if step < line - 1:
                @pl.when(has_right)
                def _():
                    hand_on(0, step, block, g, right).start()

        @pl.when(due_right)
        def _():
            block = jnp.minimum(from_right, line - 1)
            hand_on(1, 0, block, g, right).wait_recv()

            if step < line - 1:
                @pl.when(has_left)
                def _():
                    hand_on(1, step, block, g, left).start()

        @pl.when(due_left)
        def _():
            acc[g] = acc[g] + of_block(jnp.maximum(from_left, 0), g)

        @pl.when(due_right)
        def _():
            acc[g] = acc[g] + of_block(jnp.minimum(from_right, line - 1), g)

    for step in range(1, line):
        @pl.loop(0, groups - 1 if step == line - 1 else groups)
        def _(g):
            visit(step, g)

        if step == 1 and extra:
            for at_end, block, way, beside in ((is_first, 1, 1, right), (is_last, line - 2, 0, left)):
                @pl.when(at_end)
                def _():
                    hand_part(way, block, beside).wait_recv()
                    acc[whole] = acc[whole] + of_block(block, whole, rest)

    def finish(g):
        tile = combine(acc[g])
        if g < whole:
            return tile
        slot = lent if g < kept else g - kept
        acc[g, :rows] = tile

        @pl.when(is_first | is_last)
        def _():
            give_back(slot, right).wait_recv()
            acc[g, :rows] = acc[g, :rows] + back_in[slot]

        return acc[g, :rows]

    def exchange(part, source, target):
        copies = []
        for hop in range(1, across):
            other = lax.rem(mine + hop, across)
            copies.append(pltpu.make_async_remote_copy(
                src_ref=source.at[other], dst_ref=target.at[mine],
                send_sem=x_send.at[part, hop], recv_sem=x_recv.at[part, hop],
                device_id={"freq": other}, device_id_type=MESH,
            ))
        copies.append(pltpu.make_async_copy(source.at[mine], target.at[mine], x_local.at[part]))
        return copies

    def transform(source, first):
        parts = []
        for m in range(2 * per):
            lanes = [source[r, :, m * focal:(m + 1) * focal] for r in range(owned)]
            parts.append(jnp.concatenate(lanes, axis=1))
        values = jnp.concatenate(parts, axis=0)
        high = values.astype(jnp.bfloat16)
        low = (values - high.astype(jnp.float32)).astype(jnp.bfloat16)
        span = slice(first, first + values.shape[0])

        def dot(a, b):
            return lax.dot_general(a, b, (((0,), (0,)), ((), ())), preferred_element_type=jnp.float32)

        return dot(high, table[0, span]) + (dot(low, table[0, span]) + dot(high, table[1, span]))

    for g in range(groups - 1):
        tile = finish(g)
        for d in range(across):
            early_out[d, g * owned:(g + 1) * owned, :] = tile[d * owned:(d + 1) * owned]
    early = exchange(0, early_out, early_in)
    for copy in early:
        copy.start()
    early_rows[...] = jnp.zeros_like(early_rows)
    load_table.wait()
    load_onset.wait()
    load_finale.wait()
    for copy in early:
        copy.wait()
    room = early_rows.shape[1] // across
    for f in range(across):
        for r in range(owned):
            early_rows[r, f * room:f * room + groups - 1, :] = early_in[
                f, pl.ds(r, groups - 1, stride=owned), :
            ]
    traces[...] = transform(early_rows, 0)

    @pl.when(is_host)
    def _():
        for i in range(served, lent):
            serve(i)

    visit(line - 1, groups - 1)

    tile = finish(groups - 1)
    for d in range(across):
        late_out[d] = tile[d * owned:(d + 1) * owned]
    late = exchange(1, late_out, late_in)
    for copy in late:
        copy.start()
    for step in range(line - 1):
        @pl.loop(0, groups)
        def _(g):
            sent_right = own_right(g) if step == 0 else has_right & (me - step >= 0)
            sent_left = own_left(g) if step == 0 else has_left & (me + step < line)

            @pl.when(sent_right)
            def _():
                hand_on(0, step, me, g, right).wait_send()

            @pl.when(sent_left)
            def _():
                hand_on(1, step, me, g, left).wait_send()

    if extra:
        @pl.when(me == line - 2)
        def _():
            hand_part(0, me, right).wait_send()

        @pl.when(me == 1)
        def _():
            hand_part(1, me, left).wait_send()

        @pl.when(is_first | is_last)
        def _():
            lend_part(me).wait_send()

        @pl.when((me == 1) | (me == line - 2))
        def _():
            give_back(lent, right).wait_send()

    for i in range(lent):
        @pl.when(is_first | is_last)
        def _():
            lend(i, me).wait_send()

        @pl.when((me == 1) | (me == line - 2))
        def _():
            give_back(i, right).wait_send()

    for copy in late:
        copy.wait()
    for f in range(across):
        for r in range(owned):
            late_rows[r, f:f + 1, :] = late_in[f, r:r + 1, :]
    total = traces[...] + transform(late_rows, 2 * per * across * room)
    samples = lax.broadcasted_iota(jnp.int32, (focal, NT), 1)
    starts, ends = jnp.transpose(onset[...]), jnp.transpose(finale[...])
    for r in range(owned):
        inside = (samples >= starts[:, r:r + 1]) & (samples < ends[:, r:r + 1])
        windowed = jnp.where(inside, total[r * focal:(r + 1) * focal], 0.0)
        for q in range(focal):
            out_ref[q, r:r + 1, :] = windowed[q:q + 1]


def per_device(line, across, response, focusing, window_onset, window_end):
    _, freqs, rows, sources = response.shape
    focal, depth = focusing.shape[2], focusing.shape[3]
    per = LANES // (2 * focal)
    groups = freqs // per
    owned = rows // across
    lent, extra = divmod(lent_freqs(line, freqs, rows, focal), per)
    slots = lent + 1
    room = -(-(groups - 1) // 8) * 8
    tables = make_tables(across, groups, per, room)
    dma = pltpu.SemaphoreType.DMA
    return pl.pallas_call(
        functools.partial(spectra_kernel, line, across, lent, extra),
        out_shape=pltpu.VMEM((focal, owned, NT), jnp.float32),
        in_specs=[pl.BlockSpec(memory_space=pl.ANY)] * 5,
        out_specs=pl.BlockSpec(memory_space=pltpu.VMEM),
        scratch_shapes=[
            pltpu.VMEM(response.shape, jnp.bfloat16),
            pltpu.VMEM(focusing.shape, jnp.float32),
            pltpu.VMEM((line, freqs, 2 * focal, depth), jnp.bfloat16),
            pltpu.VMEM((slots, 2, per, rows, depth), jnp.bfloat16),
            pltpu.VMEM((groups, 2 * rows, LANES), jnp.float32),
            pltpu.VMEM((slots, rows, LANES), jnp.float32),
            pltpu.VMEM((slots, rows, LANES), jnp.float32),
            pltpu.VMEM(tables.shape, jnp.bfloat16),
            pltpu.VMEM((owned, focal), jnp.int32),
            pltpu.VMEM((owned, focal), jnp.int32),
            pltpu.VMEM((owned * focal, NT), jnp.float32),
            pltpu.VMEM((across, (groups - 1) * owned, LANES), jnp.float32),
            pltpu.VMEM((across, (groups - 1) * owned, LANES), jnp.float32),
            pltpu.VMEM((owned, across * room, LANES), jnp.float32),
            pltpu.VMEM((across, owned, LANES), jnp.float32),
            pltpu.VMEM((across, owned, LANES), jnp.float32),
            pltpu.VMEM((owned, across, LANES), jnp.float32),
            dma((groups,)),
            dma((groups,)),
            dma,
            dma,
            dma,
            dma((2, max(line - 1, 1), groups)),
            dma((line, groups)),
            dma((slots,)),
            dma((slots,)),
            dma((slots,)),
            dma((slots,)),
            dma((2, across)),
            dma((2, across)),
            dma((2,)),
        ],
        compiler_params=pltpu.CompilerParams(
            collective_id=0, has_side_effects=True, vmem_limit_bytes=60000 * 1024
        ),
    )(response, focusing, tables, window_onset.T, window_end.T)


def solution(mesh):
    line, across = mesh.shape["recv"], mesh.shape["freq"]
    in_specs = (
        P(None, "freq", "recv", None),
        P(None, "freq", None, "recv"),
        P(None, ("recv", "freq")),
        P(None, ("recv", "freq")),
    )
    out_specs = P(None, ("recv", "freq"), None)
    return jax.shard_map(
        functools.partial(per_device, line, across),
        mesh=mesh, in_specs=in_specs, out_specs=out_specs, check_vma=False,
    )
```

```python
import functools
import math

import jax
import jax.numpy as jnp
import numpy as np
from jax import lax
from jax.experimental import pallas as pl
from jax.experimental.pallas import tpu as pltpu
from jax.sharding import PartitionSpec as P

NT = 1024
LANES = 128
MESH = pl.DeviceIdType.MESH


def make_tables(across, groups, per, room):
    freqs = groups * per
    count = across * freqs
    phase = (np.arange(count)[:, None] * np.arange(NT)[None, :] % NT) * (2.0 * math.pi / NT)
    scale = 1.0 / math.sqrt(count)
    table = np.stack([np.cos(phase) * scale, -np.sin(phase) * scale], 1)
    table = table.reshape(across, groups, per, 2, NT).transpose(2, 3, 0, 1, 4)
    early = np.zeros((per, 2, across, room, NT))
    early[:, :, :, :groups - 1] = table[:, :, :, :groups - 1]
    both = np.concatenate([early.reshape(-1, NT), table[:, :, :, groups - 1].reshape(-1, NT)])
    high = both.astype(np.float32).astype(jnp.bfloat16)
    low = (both - high.astype(np.float64)).astype(np.float32).astype(jnp.bfloat16)
    return np.stack([high, low])


def lent_freqs(line, freqs, rows, focal):
    if line < 4:
        return 0
    return min(freqs, (line - 2) * freqs * focal // (focal + rows))


def spectra_kernel(
    line, across, lent, extra, resp_hbm, focus_hbm, table_hbm, onset_hbm, end_hbm, out_ref,
    resp, focus, held, guest, acc, back_out, back_in, table, onset, finale, traces,
    early_out, early_in, early_rows, late_out, late_in, late_rows,
    resp_sem, focus_sem, table_sem, onset_sem, finale_sem, send_sem, recv_sem, guest_send, guest_recv,
    back_send, back_recv, x_send, x_recv, x_local,
):
    me = lax.axis_index("recv")
    mine = lax.axis_index("freq")
    _, freqs, rows, _ = resp_hbm.shape
    focal, depth = focus_hbm.shape[2], focus_hbm.shape[3]
    groups = acc.shape[0]
    per = freqs // groups
    owned = rows // across
    kept = groups - lent
    whole = kept - 1 if extra else kept
    rest = per - extra
    has_left, has_right = me > 0, me < line - 1
    is_first, is_last = me == 0, me == line - 1
    left, right = jnp.maximum(me - 1, 0), jnp.minimum(me + 1, line - 1)

    def load_focus(g):
        return pltpu.make_async_copy(
            focus_hbm.at[:, pl.ds(g * per, per)], focus.at[:, pl.ds(g * per, per)], focus_sem.at[g]
        )

    def load_resp(g):
        return pltpu.make_async_copy(
            resp_hbm.at[:, pl.ds(g * per, per)], resp.at[:, pl.ds(g * per, per)], resp_sem.at[g]
        )

    barrier = pltpu.get_barrier_semaphore()

    @pl.when(has_left)
    def _():
        pl.semaphore_signal(barrier, inc=1, device_id={"recv": left}, device_id_type=MESH)

    @pl.when(has_right)
    def _():
        pl.semaphore_signal(barrier, inc=1, device_id={"recv": right}, device_id_type=MESH)

    for hop in range(1, across):
        other = lax.rem(mine + hop, across)
        pl.semaphore_signal(barrier, inc=1, device_id={"freq": other}, device_id_type=MESH)

    for g in range(groups):
        load_focus(g).start()
    for g in range(groups):
        load_resp(g).start()

    load_table = pltpu.make_async_copy(table_hbm, table, table_sem)
    load_table.start()
    load_onset = pltpu.make_async_copy(onset_hbm, onset, onset_sem)
    load_onset.start()
    load_finale = pltpu.make_async_copy(end_hbm, finale, finale_sem)
    load_finale.start()

    def convert(g):
        load_focus(g).wait()
        for i in range(per):
            k = g * per + i
            for part in range(2):
                held[me, k, part * focal:(part + 1) * focal, :] = focus[part, k].astype(jnp.bfloat16)

    for g in range(min(2, groups)):
        convert(g)

    beside = has_left.astype(jnp.int32) + has_right.astype(jnp.int32)
    pl.semaphore_wait(barrier, across - 1 + beside)

    def hand_on(way, step, block, g, target):
        piece = held.at[block, pl.ds(g * per, per)]
        return pltpu.make_async_remote_copy(
            src_ref=piece, dst_ref=piece,
            send_sem=send_sem.at[way, step, g], recv_sem=recv_sem.at[block, g],
            device_id={"recv": target}, device_id_type=MESH,
        )

    def hand_part(way, block, target):
        piece = held.at[block, pl.ds(whole * per, rest)]
        return pltpu.make_async_remote_copy(
            src_ref=piece, dst_ref=piece,
            send_sem=send_sem.at[way, 0, whole], recv_sem=recv_sem.at[block, whole],
            device_id={"recv": target}, device_id_type=MESH,
        )

    def own_right(g):
        return has_right & ((me < line - 2) | (g < whole)) if lent + extra else has_right

    def own_left(g):
        return has_left & ((me > 1) | (g < whole)) if lent + extra else has_left

    def lend(i, target):
        columns = pl.ds(pl.multiple_of(target * depth, LANES), depth)
        return pltpu.make_async_remote_copy(
            src_ref=resp.at[:, pl.ds((kept + i) * per, per), :, columns], dst_ref=guest.at[i],
            send_sem=guest_send.at[i], recv_sem=guest_recv.at[i],
            device_id={"recv": target}, device_id_type=MESH,
        )

    def lend_part(target):
        columns = pl.ds(pl.multiple_of(target * depth, LANES), depth)
        return pltpu.make_async_remote_copy(
            src_ref=resp.at[:, pl.ds(whole * per + rest, extra), :, columns],
            dst_ref=guest.at[lent, :, pl.ds(0, extra)],
            send_sem=guest_send.at[lent], recv_sem=guest_recv.at[lent],
            device_id={"recv": target}, device_id_type=MESH,
        )

    def give_back(i, target):
        return pltpu.make_async_remote_copy(
            src_ref=back_out.at[i], dst_ref=back_in.at[i],
            send_sem=back_send.at[i], recv_sem=back_recv.at[i],
            device_id={"recv": target}, device_id_type=MESH,
        )

    @pl.loop(0, groups)
    def _(g):
        @pl.when(own_right(g))
        def _():
            hand_on(0, 0, me, g, right).start()

        @pl.when(own_left(g))
        def _():
            hand_on(1, 0, me, g, left).start()

        @pl.when(g + 2 < groups)
        def _():
            convert(g + 2)

    if extra:
        @pl.when(me == line - 2)
        def _():
            hand_part(0, me, right).start()

        @pl.when(me == 1)
        def _():
            hand_part(1, me, left).start()

    def products(left_of, block, g, first=0, last=per):
        parts = []
        for i in range(per):
            if not first <= i < last:
                parts.append(jnp.zeros((2 * rows, 2 * focal), jnp.float32))
                continue
            lhs = left_of(i).reshape(2 * rows, depth)
            parts.append(
                lax.dot_general(
                    lhs, held[block, g * per + i], (((1,), (1,)), ((), ())),
                    preferred_element_type=jnp.float32,
                )
            )
        return jnp.concatenate(parts, axis=1)

    def of_block(block, g, last=per):
        columns = pl.ds(pl.multiple_of(block * depth, LANES), depth)
        return products(lambda i: resp[:, g * per + i, :, columns], block, g, 0, last)

    @pl.loop(0, groups)
    def _(g):
        load_resp(g).wait()

    if extra:
        @pl.when(is_first)
        def _():
            lend_part(right).start()

        @pl.when(is_last)
        def _():
            lend_part(left).start()

    for i in range(lent):
        @pl.when(is_first)
        def _():
            lend(i, right).start()

        @pl.when(is_last)
        def _():
            lend(i, left).start()

    @pl.loop(0, groups)
    def _(g):
        acc[g] = of_block(me, g)

    half = lax.rem(lax.broadcasted_iota(jnp.int32, (rows, LANES), 1), 2 * focal) < focal

    def combine(tile):
        real, imag = tile[:rows], tile[rows:]
        return real + jnp.where(
            half, -pltpu.roll(imag, LANES - focal, axis=1), pltpu.roll(imag, focal, axis=1)
        )

    is_host = ((me == 1) | (me == line - 2)) if lent + extra else False
    end = jnp.where(me == 1, 0, line - 1)
    served = min(lent, groups // 2)

    def serve(i):
        lend(i, end).wait_recv()
        back_out[i] = combine(products(lambda n: guest[i, :, n], me, kept + i))
        give_back(i, end).start()

    def visit(step, g):
        from_left, from_right = me - step, me + step
        if step == line - 2 and extra:
            @pl.when(is_host & (g == 0))
            def _():
                lend_part(end).wait_recv()
                tile = products(lambda n: guest[lent, :, n - rest], me, whole, rest)
                back_out[lent] = combine(tile)
                give_back(lent, end).start()

        if step == line - 2 and served:
            @pl.when(is_host & (g > 0) & (g % 2 == 0) & (g // 2 - 1 < min(served, groups // 2 - 1)))
            def _():
                serve(g // 2 - 1)

            if served == groups // 2:
                @pl.when(is_host & (g == groups - 1))
                def _():
                    serve(served - 1)

        due_left, due_right = from_left >= 0, from_right < line
        if step == 1 and lent + extra:
            due_left = due_left & ((me < line - 1) | (g < whole))
            due_right = due_right & ((me > 0) | (g < whole))

        @pl.when(due_left)
        def _():
            block = jnp.maximum(from_left, 0)
            hand_on(0, 0, block, g, left).wait_recv()

            if step < line - 1:
                @pl.when(has_right)
                def _():
                    hand_on(0, step, block, g, right).start()

        @pl.when(due_right)
        def _():
            block = jnp.minimum(from_right, line - 1)
            hand_on(1, 0, block, g, right).wait_recv()

            if step < line - 1:
                @pl.when(has_left)
                def _():
                    hand_on(1, step, block, g, left).start()

        @pl.when(due_left)
        def _():
            acc[g] = acc[g] + of_block(jnp.maximum(from_left, 0), g)

        @pl.when(due_right)
        def _():
            acc[g] = acc[g] + of_block(jnp.minimum(from_right, line - 1), g)

    for step in range(1, line):
        @pl.loop(0, groups - 1 if step == line - 1 else groups)
        def _(g):
            visit(step, g)

        if step == 1 and extra:
            for at_end, block, way, beside in ((is_first, 1, 1, right), (is_last, line - 2, 0, left)):
                @pl.when(at_end)
                def _():
                    hand_part(way, block, beside).wait_recv()
                    acc[whole] = acc[whole] + of_block(block, whole, rest)

    def finish(g):
        tile = combine(acc[g])
        if g < whole:
            return tile
        slot = lent if g < kept else g - kept
        acc[g, :rows] = tile

        @pl.when(is_first | is_last)
        def _():
            give_back(slot, right).wait_recv()
            acc[g, :rows] = acc[g, :rows] + back_in[slot]

        return acc[g, :rows]

    def exchange(part, source, target):
        copies = []
        for hop in range(1, across):
            other = lax.rem(mine + hop, across)
            copies.append(pltpu.make_async_remote_copy(
                src_ref=source.at[other], dst_ref=target.at[mine],
                send_sem=x_send.at[part, hop], recv_sem=x_recv.at[part, hop],
                device_id={"freq": other}, device_id_type=MESH,
            ))
        copies.append(pltpu.make_async_copy(source.at[mine], target.at[mine], x_local.at[part]))
        return copies

    def transform(source, first):
        parts = []
        for m in range(2 * per):
            lanes = [source[r, :, m * focal:(m + 1) * focal] for r in range(owned)]
            parts.append(jnp.concatenate(lanes, axis=1))
        values = jnp.concatenate(parts, axis=0)
        high = values.astype(jnp.bfloat16)
        low = (values - high.astype(jnp.float32)).astype(jnp.bfloat16)
        span = slice(first, first + values.shape[0])

        def dot(a, b):
            return lax.dot_general(a, b, (((0,), (0,)), ((), ())), preferred_element_type=jnp.float32)

        return dot(high, table[0, span]) + (dot(low, table[0, span]) + dot(high, table[1, span]))

    for g in range(groups - 1):
        tile = finish(g)
        for d in range(across):
            early_out[d, g * owned:(g + 1) * owned, :] = tile[d * owned:(d + 1) * owned]
    early = exchange(0, early_out, early_in)
    for copy in early:
        copy.start()
    early_rows[...] = jnp.zeros_like(early_rows)
    load_table.wait()
    load_onset.wait()
    load_finale.wait()
    for copy in early:
        copy.wait()
    room = early_rows.shape[1] // across
    for f in range(across):
        for r in range(owned):
            early_rows[r, f * room:f * room + groups - 1, :] = early_in[
                f, pl.ds(r, groups - 1, stride=owned), :
            ]
    traces[...] = transform(early_rows, 0)

    @pl.when(is_host)
    def _():
        for i in range(served, lent):
            serve(i)

    visit(line - 1, groups - 1)

    tile = finish(groups - 1)
    for d in range(across):
        late_out[d] = tile[d * owned:(d + 1) * owned]
    late = exchange(1, late_out, late_in)
    for copy in late:
        copy.start()
    for step in range(line - 1):
        @pl.loop(0, groups)
        def _(g):
            sent_right = own_right(g) if step == 0 else has_right & (me - step >= 0)
            sent_left = own_left(g) if step == 0 else has_left & (me + step < line)

            @pl.when(sent_right)
            def _():
                hand_on(0, step, me, g, right).wait_send()

            @pl.when(sent_left)
            def _():
                hand_on(1, step, me, g, left).wait_send()

    if extra:
        @pl.when(me == line - 2)
        def _():
            hand_part(0, me, right).wait_send()

        @pl.when(me == 1)
        def _():
            hand_part(1, me, left).wait_send()

        @pl.when(is_first | is_last)
        def _():
            lend_part(me).wait_send()

        @pl.when((me == 1) | (me == line - 2))
        def _():
            give_back(lent, right).wait_send()

    for i in range(lent):
        @pl.when(is_first | is_last)
        def _():
            lend(i, me).wait_send()

        @pl.when((me == 1) | (me == line - 2))
        def _():
            give_back(i, right).wait_send()

    samples = lax.broadcasted_iota(jnp.int32, (focal, NT), 1)
    starts, ends = jnp.transpose(onset[...]), jnp.transpose(finale[...])
    for copy in late:
        copy.wait()
    for f in range(across):
        for r in range(owned):
            late_rows[r, f:f + 1, :] = late_in[f, r:r + 1, :]
    total = traces[...] + transform(late_rows, 2 * per * across * room)
    for r in range(owned):
        inside = (samples >= starts[:, r:r + 1]) & (samples < ends[:, r:r + 1])
        windowed = jnp.where(inside, total[r * focal:(r + 1) * focal], 0.0)
        for q in range(focal):
            out_ref[q, r:r + 1, :] = windowed[q:q + 1]


def per_device(line, across, response, focusing, window_onset, window_end):
    _, freqs, rows, sources = response.shape
    focal, depth = focusing.shape[2], focusing.shape[3]
    per = LANES // (2 * focal)
    groups = freqs // per
    owned = rows // across
    lent, extra = divmod(lent_freqs(line, freqs, rows, focal), per)
    slots = lent + 1
    room = -(-(groups - 1) // 8) * 8
    tables = make_tables(across, groups, per, room)
    dma = pltpu.SemaphoreType.DMA
    return pl.pallas_call(
        functools.partial(spectra_kernel, line, across, lent, extra),
        out_shape=pltpu.VMEM((focal, owned, NT), jnp.float32),
        in_specs=[pl.BlockSpec(memory_space=pl.ANY)] * 5,
        out_specs=pl.BlockSpec(memory_space=pltpu.VMEM),
        scratch_shapes=[
            pltpu.VMEM(response.shape, jnp.bfloat16),
            pltpu.VMEM(focusing.shape, jnp.float32),
            pltpu.VMEM((line, freqs, 2 * focal, depth), jnp.bfloat16),
            pltpu.VMEM((slots, 2, per, rows, depth), jnp.bfloat16),
            pltpu.VMEM((groups, 2 * rows, LANES), jnp.float32),
            pltpu.VMEM((slots, rows, LANES), jnp.float32),
            pltpu.VMEM((slots, rows, LANES), jnp.float32),
            pltpu.VMEM(tables.shape, jnp.bfloat16),
            pltpu.VMEM((owned, focal), jnp.int32),
            pltpu.VMEM((owned, focal), jnp.int32),
            pltpu.VMEM((owned * focal, NT), jnp.float32),
            pltpu.VMEM((across, (groups - 1) * owned, LANES), jnp.float32),
            pltpu.VMEM((across, (groups - 1) * owned, LANES), jnp.float32),
            pltpu.VMEM((owned, across * room, LANES), jnp.float32),
            pltpu.VMEM((across, owned, LANES), jnp.float32),
            pltpu.VMEM((across, owned, LANES), jnp.float32),
            pltpu.VMEM((owned, across, LANES), jnp.float32),
            dma((groups,)),
            dma((groups,)),
            dma,
            dma,
            dma,
            dma((2, max(line - 1, 1), groups)),
            dma((line, groups)),
            dma((slots,)),
            dma((slots,)),
            dma((slots,)),
            dma((slots,)),
            dma((2, across)),
            dma((2, across)),
            dma((2,)),
        ],
        compiler_params=pltpu.CompilerParams(
            collective_id=0, has_side_effects=True, vmem_limit_bytes=60000 * 1024
        ),
    )(response, focusing, tables, window_onset.T, window_end.T)


def solution(mesh):
    line, across = mesh.shape["recv"], mesh.shape["freq"]
    in_specs = (
        P(None, "freq", "recv", None),
        P(None, "freq", None, "recv"),
        P(None, ("recv", "freq")),
        P(None, ("recv", "freq")),
    )
    out_specs = P(None, ("recv", "freq"), None)
    return jax.shard_map(
        functools.partial(per_device, line, across),
        mesh=mesh, in_specs=in_specs, out_specs=out_specs, check_vma=False,
    )
```
